32 devices in a mesh: head: 4 (over x, core), seq: 8 (over z, y).
Axes of the slice: x: 2, y: 2, z: 4, core: 2. Of those that a mesh axis runs over, the one named last changes fastest.
Arguments:
- queries: bfloat16 [2048, 4096], P('seq', 'head'), may hold values from -160 to 160
- encodings: bfloat16 [24, 128, 1024], P('seq', None, 'head'), may hold values from -6 to 6
- kv_weight: bfloat16 [2, 1024, 4096], P(None, None, 'head'), may hold values from -0.1875 to 0.1875
- grad_out: bfloat16 [2048, 4096], P('seq', 'head'), may hold values from -6 to 6
- neighbour_owner: int32 [32, 2], replicated, may hold values from 0 to 7, all different within a row; in each aligned block of 4 rows (0 to 3, 4 to 7, ...) at most 2 rows name the same one
- neighbour_slot: int32 [32, 2], replicated, may hold values from 0 to 2
Outputs:
- attended: bfloat16 [2048, 4096], P('seq', 'head')
- query_grad: bfloat16 [32, 64, 4096], P('seq', 'head')
- encoding_grad: bfloat16 [24, 128, 1024], P('seq', None, 'head')
The draws below stay inside these ranges and needn't reach their ends.
Inputs may be any that keep to these rules, and one draw needn't show every extreme that they name: `neighbour_owner`: the 2 owners of one span differ. Among the 4 spans of one index of seq (aligned blocks of rows), no owner is named more than 2 times, and in every draw some owner is named exactly 2 times.
All inputs are finite; a program needn't handle non-finite values.
Results may differ from the reference program's by a relative error of at most 0.019.
The reference program's roundings to bfloat16 on the way count: a program that leaves them out, or rounds other values in their place, can miss the bound.
Values may be sent and summed in bfloat16 or wider, within the bound.
A program may use at most 64 MiB of HBM per device.

```python
import math
import jax
import jax.numpy as jnp
import numpy as np
from jax import lax

HEADS = 32
HEAD_DIM = 128
D = 4096
ENC_WIDTH = 1024
SPAN = 64
NEIGHBOURS = 2
NEIGHBOUR_LEN = 128
SPANS_DEV = 4
TILES_DEV = 3
CAPACITY = 2
SPANS = 32
TOKENS = 2048
NTILES = 24
N_SEQ = 8


def draw_queries(key, part):
    base = jax.random.normal(jax.random.fold_in(key, 11), (TOKENS, D), jnp.float32)
    base = jnp.clip(base, -4.0, 4.0)
    return base.astype(jnp.bfloat16)


def touch_ends(values, stream_key, smallest, largest):
    extent = values.shape
    spot = [jax.random.randint(jax.random.fold_in(stream_key, axis), (), 0, extent[axis]) for axis in range(len(extent))]
    values = values.at[tuple(spot)].set(smallest)
    longest = extent.index(max(extent))
    spot[longest] = (spot[longest] + 1) % extent[longest]
    return values.at[tuple(spot)].set(largest)


def steps_of(own_key, dims, pieces, smallest, top_value):
    factor_of, own = 1.0, jax.random.fold_in(own_key, 6)
    for axis_at, shards_of in pieces:
        draws = jnp.exp(jax.random.uniform(jax.random.fold_in(own, axis_at), (shards_of,), jnp.float32, smallest / len(pieces), top_value / len(pieces)))
        factor_of = factor_of * jnp.repeat(draws, dims[axis_at] // shards_of).reshape([-1 if axis == axis_at else 1 for axis in range(len(dims))])
    return factor_of


def assign_block(key, own, number, rows, amount, top, limit, slope):
    order = jax.random.permutation(key, amount)
    heavy_load, usual = shares(amount, rows * top, limit, slope, True), shares(amount, rows * top, limit, slope, False)
    places = jnp.arange(amount)

    def named(lengths, turn):
        used = int((lengths > 0).sum())
        fixed = max(1, used // 4)
        shifted = fixed + (places - fixed + turn * (used - fixed)) % max(1, amount - fixed)
        return jnp.zeros((amount,), jnp.int32).at[order[jnp.where(places < fixed, places, shifted)]].set(jnp.asarray(lengths, jnp.int32))

    lengths = jnp.where(number % 4 == 0, named(heavy_load, number // 4), named(usual, number - number // 4 - 1))
    mixed = jax.random.permutation(jax.random.fold_in(own, 3), amount)
    source_of, taker = mixed[0:amount // 2 * 2:2], mixed[1:amount // 2 * 2:2]
    slack = jnp.minimum(lengths[source_of] - 1, limit - lengths[taker]) // 2
    slack = jnp.where((source_of == order[0]) | (taker == order[0]) | (lengths[taker] == 0), 0, jnp.maximum(slack, 0))
    shifted = jax.random.randint(jax.random.fold_in(own, 4), (amount // 2,), 0, 1 << 20) % (slack + 1)
    lengths = lengths.at[source_of].add(-shifted).at[taker].add(shifted)
    members = jnp.searchsorted(jnp.cumsum(lengths), jnp.arange(rows * top), side="right").astype(jnp.int32)
    grid = members.reshape(top, rows).T
    grid = grid[jax.random.permutation(jax.random.fold_in(own, 1), rows)]
    turn = jax.random.randint(jax.random.fold_in(own, 2), (rows, 1), 0, top)
    return jnp.take_along_axis(grid, (jnp.arange(top)[None, :] + turn) % top, axis=1)


def shares(number_of, total, bound, skew, full):
    loads = [(1 << 20) // math.isqrt(grade ** skew) + 1 for grade in range(1, number_of + 1)]
    largest = bound if full else min(bound, max(-(-total // number_of), total * loads[0] // sum(loads)))
    least = 1 if total - largest >= number_of - 1 else 0
    holding, surplus = [largest] + [least] * (number_of - 1), total - largest - least * (number_of - 1)
    while surplus > 0:
        candidates = [i for i in range(1, number_of) if holding[i] < largest] or [i for i in range(1, number_of) if holding[i] < bound]
        whole, budget = sum([loads[i] for i in candidates]), surplus
        for i in candidates:
            extra = min(bound - holding[i], max(1, budget * loads[i] // whole), surplus)
            holding[i] = holding[i] + extra
            surplus = surplus - extra
    return np.array(holding)


def gaussian(key, extent, width, reach, split=(), held_as=jnp.bfloat16):
    result = jax.random.normal(key, extent, jnp.float32) * width
    if len(split) > 0:
        result = steps_of(key, extent, split, -0.22, 0.18) * result
    return jnp.clip(result, min=-reach, max=reach).astype(held_as)


def setup_inputs(seed: int = 0) -> dict:
    key_of = jax.random.split(jax.random.key(seed), 7)
    queries = draw_queries(jax.random.fold_in(key_of[6], 71), 0)
    encodings = gaussian(key_of[1], (NTILES, NEIGHBOUR_LEN, ENC_WIDTH), 1.0, 6.0, ((0, 8), (2, 4)))
    kv_weight = gaussian(key_of[2], (2, ENC_WIDTH, D), ENC_WIDTH ** -0.5, 0.1875, ((2, 4),))
    grad_out = gaussian(key_of[3], (TOKENS, D), 1.0, 6.0, ((0, 8), (1, 4)))
    neighbour_owner_keys = jax.random.split(jax.random.fold_in(key_of[4], 1), SPANS // SPANS_DEV)
    neighbour_owner_turns = jax.random.permutation(jax.random.fold_in(key_of[4], 3), SPANS // SPANS_DEV)
    neighbour_owner = jax.vmap(lambda own, number: assign_block(jax.random.fold_in(key_of[4], 2), own, number, SPANS_DEV, N_SEQ, NEIGHBOURS, CAPACITY, 2))(neighbour_owner_keys, neighbour_owner_turns).reshape((SPANS, NEIGHBOURS))
    neighbour_slot = touch_ends(jax.random.randint(key_of[5], (SPANS, NEIGHBOURS), 0, TILES_DEV), jax.random.fold_in(key_of[5], 1), 0, TILES_DEV - 1).astype(jnp.int32)
    return dict(queries=queries, encodings=encodings, kv_weight=kv_weight, grad_out=grad_out, neighbour_owner=neighbour_owner, neighbour_slot=neighbour_slot)


def round_half(values):
    return lax.optimization_barrier(values.astype(jnp.bfloat16)).astype(jnp.float32)


def reference(queries, encodings, kv_weight, grad_out, neighbour_owner, neighbour_slot):
    scale = HEAD_DIM ** -0.5
    weight_wide = kv_weight.astype(jnp.float32)
    tile_index = (neighbour_owner * TILES_DEV + neighbour_slot).astype(jnp.int32)
    tile_count = encodings.shape[0]

    def project(stored):
        return jnp.einsum("le,ced->cld", stored.astype(jnp.float32), weight_wide).astype(jnp.bfloat16)

    projected = lax.map(project, encodings)

    def grouped(rows):
        padded = jnp.concatenate([jnp.zeros((1, D), rows.dtype), rows, jnp.zeros((SPAN - 1, D), rows.dtype)], 0)
        return padded[SPAN:].reshape(SPANS, SPAN, HEADS, HEAD_DIM)

    query_groups = grouped(queries)
    grad_groups = grouped(grad_out)

    def step(total, inputs):
        query_block, grad_block, index_row = inputs
        paired = projected[index_row]
        paired = jnp.swapaxes(paired, 0, 1).reshape(2, NEIGHBOURS * NEIGHBOUR_LEN, HEADS, HEAD_DIM).astype(jnp.float32)
        query_wide = query_block.astype(jnp.float32)
        grad_wide = grad_block.astype(jnp.float32)
        scores = jnp.einsum("qhd,khd->hqk", query_wide, paired[0]) * scale
        top = jnp.max(scores, axis=-1, keepdims=True)
        expo = jnp.exp(scores - top)
        probs = expo / jnp.sum(expo, axis=-1, keepdims=True)
        probs_half = round_half(probs)
        output = jnp.einsum("hqk,khd->qhd", probs_half, paired[1]).astype(jnp.bfloat16)
        dprob = jnp.einsum("qhd,khd->hqk", grad_wide, paired[1])
        delta = jnp.sum(probs * dprob, axis=-1, keepdims=True)
        dscore = round_half(probs * (dprob - delta))
        qgrad = jnp.einsum("hqk,khd->qhd", dscore, paired[0]) * scale
        kgrad = jnp.einsum("hqk,qhd->khd", dscore, query_wide) * scale
        vgrad = jnp.einsum("hqk,qhd->khd", probs_half, grad_wide)
        grads = jnp.stack([kgrad, vgrad], 0).reshape(2, NEIGHBOURS, NEIGHBOUR_LEN, D)
        grads = round_half(jnp.swapaxes(grads, 0, 1))
        total = total.at[index_row].add(grads)
        return total, (output, qgrad)

    init = jnp.zeros((tile_count, 2, NEIGHBOUR_LEN, D), jnp.float32)
    total, (outputs, qgrads) = lax.scan(step, init, (query_groups, grad_groups, tile_index))
    flat_out = outputs.reshape(SPANS * SPAN, D)[: TOKENS - SPAN + 1]
    attended = jnp.concatenate([jnp.zeros((SPAN - 1, D), jnp.bfloat16), flat_out], 0)
    flat_grad = qgrads.reshape(SPANS * SPAN, D)[: TOKENS - SPAN + 1]
    query_grad = jnp.concatenate([jnp.zeros((SPAN - 1, D), jnp.float32), flat_grad], 0)
    query_grad = query_grad.astype(jnp.bfloat16).reshape(SPANS, SPAN, D)

    def back_project(summed):
        return jnp.einsum("cld,ced->le", summed, weight_wide, precision=lax.Precision.HIGHEST)

    encoding_grad = lax.map(back_project, total).astype(jnp.bfloat16)
    return attended, query_grad, encoding_grad
```

```python
import functools

import jax
import jax.numpy as jnp
from jax import lax
from jax.experimental import pallas as pl
from jax.experimental.pallas import tpu as pltpu
from jax.sharding import PartitionSpec as P

HEAD_DIM = 128
SPAN = 64
NEIGHBOURS = 2
NEIGHBOUR_LEN = 128
WINDOW = NEIGHBOURS * NEIGHBOUR_LEN
SCALE = HEAD_DIM ** (-0.5)
F32 = jnp.float32
BF16 = jnp.bfloat16


def dot(a, b, da, db):
    return lax.dot_general(a, b, (((da,), (db,)), ((), ())), preferred_element_type=F32)


def group_body(feat_ref, weight_ref, query_ref, grad_ref, att_ref, qgrad_ref, term_ref, kv, kv_grad):
    parts, _, part = feat_ref.shape
    width = query_ref.shape[1]
    for c in range(2):
        total = None
        for j in range(parts):
            piece = dot(feat_ref[j], weight_ref[c, j * part : (j + 1) * part, :], 1, 0)
            total = piece if total is None else total + piece
        kv[c] = total.astype(BF16)
    for h in range(width // HEAD_DIM):
        cols = slice(h * HEAD_DIM, (h + 1) * HEAD_DIM)
        q = query_ref[:, cols]
        g = grad_ref[:, cols]
        k = kv[0, :, cols]
        v = kv[1, :, cols]
        scores = dot(q, k, 1, 1) * SCALE
        dprob = dot(g, v, 1, 1)
        expo = jnp.exp(scores - jnp.max(scores, axis=-1, keepdims=True))
        probs = expo / jnp.sum(expo, axis=-1, keepdims=True)
        half = probs.astype(BF16)
        delta = jnp.sum(probs * dprob, axis=-1, keepdims=True)
        dscore = (probs * (dprob - delta)).astype(BF16)
        att_ref[:, cols] = dot(half, v, 1, 0).astype(BF16)
        qgrad_ref[:, cols] = (dot(dscore, k, 1, 0) * SCALE).astype(BF16)
        kv_grad[0, :, cols] = (dot(dscore, q, 0, 0) * SCALE).astype(BF16)
        kv_grad[1, :, cols] = dot(half, g, 0, 0).astype(BF16)
    for j in range(parts):
        rows = slice(j * part, (j + 1) * part)
        term_ref[j] = dot(kv_grad[0], weight_ref[0, rows, :], 1, 1) + dot(
            kv_grad[1], weight_ref[1, rows, :], 1, 1
        )


def run_groups(features, kv_weight, query_rows, grad_rows):
    parts, rows, part = features.shape
    token_rows, width = query_rows.shape
    groups = token_rows // SPAN
    token_spec = pl.BlockSpec((SPAN, width), lambda i: (i, 0))
    return pl.pallas_call(
        group_body,
        grid=(groups,),
        in_specs=[
            pl.BlockSpec((parts, WINDOW, part), lambda i: (0, i, 0)),
            pl.BlockSpec(kv_weight.shape, lambda i: (0, 0, 0), pipeline_mode=pl.Buffered(1)),
            token_spec,
            token_spec,
        ],
        out_specs=[
            token_spec,
            token_spec,
            pl.BlockSpec((parts, WINDOW, part), lambda i: (0, i, 0)),
        ],
        out_shape=[
            jax.ShapeDtypeStruct((token_rows, width), BF16),
            jax.ShapeDtypeStruct((token_rows, width), BF16),
            jax.ShapeDtypeStruct((parts, rows, part), F32),
        ],
        scratch_shapes=[
            pltpu.VMEM((2, WINDOW, width), BF16),
            pltpu.VMEM((2, WINDOW, width), BF16),
        ],
        compiler_params=pltpu.CompilerParams(
            dimension_semantics=("arbitrary",), vmem_limit_bytes=40 << 20
        ),
    )(features, kv_weight, query_rows, grad_rows)


def per_device(queries, encodings, kv_weight, grad_out, neighbour_owner, neighbour_slot):
    seq_count = lax.axis_size("seq")
    seq_index = lax.axis_index("seq")
    token_rows, width = queries.shape
    requests = token_rows // SPAN * NEIGHBOURS
    tile_rows, _, part = encodings.shape
    forward = [(i, (i + 1) % seq_count) for i in range(seq_count)]
    backward = [((i + 1) % seq_count, i) for i in range(seq_count)]

    tile = neighbour_owner * tile_rows + neighbour_slot
    tile = jnp.roll(tile, 1, axis=0).reshape(seq_count, requests)
    tile = lax.dynamic_index_in_dim(tile, seq_index, 0, keepdims=False)

    stored = lax.all_gather(encodings, "seq", axis=0, tiled=True)
    picked = stored[tile].reshape(requests * NEIGHBOUR_LEN, part)
    features = lax.all_gather(picked, "head", axis=0, tiled=False)

    edge = jnp.stack([queries[-1:], grad_out[-1:]], 0)
    edge = lax.ppermute(edge, "seq", forward)
    row = lax.broadcasted_iota(jnp.int32, (token_rows, 1), 0)
    unattending = (seq_index == 0) & (row >= 1) & (row < SPAN)
    zero = jnp.zeros((), BF16)

    def shifted(rows, first):
        rows = jnp.concatenate([first, rows[:-1]], 0)
        return jnp.where(unattending, zero, rows)

    query_rows = shifted(queries, edge[0])
    grad_rows = shifted(grad_out, edge[1])
    att, qgrad, term = run_groups(features, kv_weight, query_rows, grad_rows)

    att = jnp.where(unattending, zero, att)
    last = lax.ppermute(jnp.stack([att[:1], qgrad[:1]], 0), "seq", backward)
    attended = jnp.concatenate([att[1:], last[0]], 0)
    qgrad = jnp.concatenate([qgrad[1:], last[1]], 0).reshape(-1, SPAN, width)
    query_grad = lax.all_to_all(qgrad, "head", split_axis=1, concat_axis=2, tiled=True)

    mine = lax.psum_scatter(term, "head", scatter_dimension=0, tiled=True)
    mine = mine.reshape(requests, NEIGHBOUR_LEN, part)
    tiles = jnp.zeros((seq_count * tile_rows, NEIGHBOUR_LEN, part), F32).at[tile].add(mine)
    total = lax.psum_scatter(tiles, "seq", scatter_dimension=0, tiled=True)
    return attended, query_grad, total.astype(BF16)


def solution(mesh):
    in_specs = (
        P("seq", "head"),
        P("seq", None, "head"),
        P(None, None, "head"),
        P("seq", "head"),
        P(),
        P(),
    )
    out_specs = (P("seq", "head"), P("seq", "head", None), P("seq", None, "head"))
    return jax.shard_map(
        per_device, mesh=mesh, in_specs=in_specs, out_specs=out_specs, check_vma=False
    )
```

```python
import functools

import jax
import jax.numpy as jnp
from jax import lax
from jax.experimental import pallas as pl
from jax.experimental.pallas import tpu as pltpu
from jax.sharding import PartitionSpec as P

HEAD_DIM = 128
SPAN = 64
NEIGHBOURS = 2
NEIGHBOUR_LEN = 128
WINDOW = NEIGHBOURS * NEIGHBOUR_LEN
SCALE = HEAD_DIM ** (-0.5)
F32 = jnp.float32
BF16 = jnp.bfloat16


def dot(a, b, da, db):
    return lax.dot_general(a, b, (((da,), (db,)), ((), ())), preferred_element_type=F32)


def ring_place(index, count):
    odd = index % 2
    return (1 - odd) * (index // 2) + odd * (count - 1 - index // 2)


def ring_index(place, count):
    place = (place + 2 * count) % count
    upper = place // (count // 2)
    return (1 - upper) * 2 * place + upper * (2 * (count - 1 - place) + 1)


def meet(axis, others):
    barrier = pltpu.get_barrier_semaphore()
    for other in others:
        pl.semaphore_signal(
            barrier, inc=1, device_id={axis: other}, device_id_type=pl.DeviceIdType.MESH
        )
    pl.semaphore_wait(barrier, len(others))


def remote(src, dst, send, recv, axis, other):
    return pltpu.make_async_remote_copy(
        src_ref=src,
        dst_ref=dst,
        send_sem=send,
        recv_sem=recv,
        device_id={axis: other},
        device_id_type=pl.DeviceIdType.MESH,
    )


def gather_body(count, shard_ref, out_ref, send, recv):
    me = lax.axis_index("seq")
    place = ring_place(me, count)
    neighbours = (ring_index(place + 1, count), ring_index(place - 1, count))
    meet("seq", neighbours)
    out_ref[me] = shard_ref[...]
    rows = shard_ref.shape[1] // 2
    hops = ((count // 2, count // 2 - 1), (count // 2 - 1, count // 2))

    def copy(way, half, step):
        owner = ring_index(place - step if way == 0 else place + step, count)
        ref = out_ref.at[owner, :, pl.ds(half * rows, rows), :]
        return remote(
            ref, ref, send.at[way, half, step], recv.at[way, half, step], "seq", neighbours[way]
        )

    lanes = [(way, half) for half in range(2) for way in range(2)]
    for step in range(count // 2):
        for way, half in lanes:
            if step < hops[way][half]:
                if step > 0:
                    copy(way, half, step - 1).wait_recv()
                copy(way, half, step).start()
    for way, half in lanes:
        copy(way, half, hops[way][half] - 1).wait_recv()
        for step in range(hops[way][half]):
            copy(way, half, step).wait_send()


def gather_tiles(shard, count):
    tiles, rows, part = shard.shape
    return pl.pallas_call(
        functools.partial(gather_body, count),
        in_specs=[pl.BlockSpec(memory_space=pltpu.VMEM)],
        out_specs=pl.BlockSpec(memory_space=pltpu.VMEM),
        out_shape=jax.ShapeDtypeStruct((count, tiles, rows, part), shard.dtype),
        scratch_shapes=[
            pltpu.SemaphoreType.DMA((2, 2, count // 2)),
            pltpu.SemaphoreType.DMA((2, 2, count // 2)),
        ],
        compiler_params=pltpu.CompilerParams(
            collective_id=0, has_side_effects=True, vmem_limit_bytes=32 << 20
        ),
    )(shard)


def scatter_body(count, share_ref, mine_ref, out_ref, buf, send, recv):
    me = lax.axis_index("seq")
    place = ring_place(me, count)
    neighbours = (ring_index(place + 1, count), ring_index(place - 1, count))
    meet("seq", neighbours)
    tiles, length, _ = out_ref.shape
    requests = mine_ref.shape[0]
    rows = length // 2

    def own(way, target, k):
        total = None
        for r in range(requests):
            piece = share_ref[target * tiles + k, r] * mine_ref[r, way * rows : (way + 1) * rows, :]
            total = piece if total is None else total + piece
        return total

    def target_of(way, step):
        return ring_index(place - 1 - step if way == 0 else place + 1 + step, count)

    def copy(way, step, k):
        return remote(
            buf.at[way, step, k],
            buf.at[way, step + 1, k],
            send.at[way, step, k],
            recv.at[way, step, k],
            "seq",
            neighbours[way],
        )

    for k in range(tiles):
        for way in range(2):
            buf[way, 0, k] = own(way, target_of(way, 0), k)
            copy(way, 0, k).start()

    def step_body(step, carry):
        for k in range(tiles):
            for way in range(2):
                piece = own(way, target_of(way, step), k)
                copy(way, step - 1, k).wait_recv()
                buf[way, step, k] = buf[way, step, k] + piece
                copy(way, step, k).start()
        return carry

    lax.fori_loop(1, count - 1, step_body, 0)
    for k in range(tiles):
        for way in range(2):
            piece = own(way, me, k)
            copy(way, count - 2, k).wait_recv()
            out_ref[k, way * rows : (way + 1) * rows, :] = (buf[way, count - 1, k] + piece).astype(
                out_ref.dtype
            )

    def drain(step, carry):
        for k in range(tiles):
            for way in range(2):
                copy(way, step, k).wait_send()
        return carry

    lax.fori_loop(0, count - 1, drain, 0)


def scatter_tiles(share, mine, count, tiles):
    _, length, part = mine.shape
    return pl.pallas_call(
        functools.partial(scatter_body, count),
        in_specs=[
            pl.BlockSpec(memory_space=pltpu.SMEM),
            pl.BlockSpec(memory_space=pltpu.VMEM),
        ],
        out_specs=pl.BlockSpec(memory_space=pltpu.VMEM),
        out_shape=jax.ShapeDtypeStruct((tiles, length, part), BF16),
        scratch_shapes=[
            pltpu.VMEM((2, count, tiles, length // 2, part), F32),
            pltpu.SemaphoreType.DMA((2, count - 1, tiles)),
            pltpu.SemaphoreType.DMA((2, count - 1, tiles)),
        ],
        compiler_params=pltpu.CompilerParams(
            collective_id=2, has_side_effects=True, vmem_limit_bytes=32 << 20
        ),
    )(share, mine)


def group_body(
    parts, feat_ref, weight_ref, query_ref, grad_ref, att_ref, qgrad_ref, out_ref,
    kv, kv_grad, term, from_core, across, from_chip, core_send, core_recv, chip_send, chip_recv,
):
    head = lax.axis_index("head")
    core, chip = head % 2, head // 2
    chips = parts // 2
    sibling = chip * 2 + 1 - core
    peers = [((chip + d) % chips) * 2 + core for d in range(1, chips)]
    meet("head", [sibling] + peers)
    part = feat_ref.shape[2]
    width = query_ref.shape[1]
    groups = query_ref.shape[0] // SPAN

    def to_core(i):
        return remote(
            term.at[i, 1 - core], from_core.at[i], core_send.at[i], core_recv.at[i], "head", sibling
        )

    def to_chip(i, d):
        return remote(
            across.at[i, d - 1],
            from_chip.at[i, d - 1],
            chip_send.at[i, d - 1],
            chip_recv.at[i, d - 1],
            "head",
            peers[d - 1],
        )

    def pass_on(i):
        to_core(i).wait_recv()
        for d in range(1, chips):
            target = (chip + d) % chips
            across[i, d - 1] = term[i, core, target] + from_core[i, target]
            to_chip(i, d).start()

    def group(i, carry):
        keys = pl.ds(pl.multiple_of(i * WINDOW, WINDOW), WINDOW)
        tokens = pl.ds(pl.multiple_of(i * SPAN, SPAN), SPAN)
        for c in range(2):
            total = None
            for j in range(parts):
                piece = dot(feat_ref[j, keys, :], weight_ref[c, j * part : (j + 1) * part, :], 1, 0)
                total = piece if total is None else total + piece
            kv[c] = total.astype(BF16)
        for h in range(width // HEAD_DIM):
            cols = slice(h * HEAD_DIM, (h + 1) * HEAD_DIM)
            q = query_ref[tokens, cols]
            g = grad_ref[tokens, cols]
            k = kv[0, :, cols]
            v = kv[1, :, cols]
            scores = dot(q, k, 1, 1) * SCALE
            dprob = dot(g, v, 1, 1)
            expo = jnp.exp(scores - jnp.max(scores, axis=-1, keepdims=True))
            probs = expo / jnp.sum(expo, axis=-1, keepdims=True)
            half = probs.astype(BF16)
            delta = jnp.sum(probs * dprob, axis=-1, keepdims=True)
            dscore = (probs * (dprob - delta)).astype(BF16)
            att_ref[tokens, cols] = dot(half, v, 1, 0).astype(BF16)
            qgrad_ref[tokens, cols] = (dot(dscore, k, 1, 0) * SCALE).astype(BF16)
            kv_grad[0, :, cols] = (dot(dscore, q, 0, 0) * SCALE).astype(BF16)
            kv_grad[1, :, cols] = dot(half, g, 0, 0).astype(BF16)
        for j in range(parts):
            rows = slice(j * part, (j + 1) * part)
            term[i, j % 2, j // 2] = dot(kv_grad[0], weight_ref[0, rows, :], 1, 1) + dot(
                kv_grad[1], weight_ref[1, rows, :], 1, 1
            )
        to_core(i).start()

        @pl.when(i > 0)
        def _():
            pass_on(i - 1)

        return carry

    lax.fori_loop(0, groups, group, 0)
    pass_on(groups - 1)
    for i in range(groups):
        total = term[i, core, chip] + from_core[i, chip]
        for d in range(1, chips):
            to_chip(i, d).wait_recv()
            total = total + from_chip[i, d - 1]
        out_ref[i * WINDOW : (i + 1) * WINDOW, :] = total
    for i in range(groups):
        to_core(i).wait_send()
        for d in range(1, chips):
            to_chip(i, d).wait_send()


def run_groups(features, kv_weight, query_rows, grad_rows):
    parts, rows, part = features.shape
    token_rows, width = query_rows.shape
    groups = token_rows // SPAN
    chips = parts // 2
    vmem = pl.BlockSpec(memory_space=pltpu.VMEM)
    return pl.pallas_call(
        functools.partial(group_body, parts),
        in_specs=[vmem] * 4,
        out_specs=[vmem] * 3,
        out_shape=[
            jax.ShapeDtypeStruct((token_rows, width), BF16),
            jax.ShapeDtypeStruct((token_rows, width), BF16),
            jax.ShapeDtypeStruct((rows, part), F32),
        ],
        scratch_shapes=[
            pltpu.VMEM((2, WINDOW, width), BF16),
            pltpu.VMEM((2, WINDOW, width), BF16),
            pltpu.VMEM((groups, 2, chips, WINDOW, part), F32),
            pltpu.VMEM((groups, chips, WINDOW, part), F32),
            pltpu.VMEM((groups, chips - 1, WINDOW, part), F32),
            pltpu.VMEM((groups, chips - 1, WINDOW, part), F32),
            pltpu.SemaphoreType.DMA((groups,)),
            pltpu.SemaphoreType.DMA((groups,)),
            pltpu.SemaphoreType.DMA((groups, chips - 1)),
            pltpu.SemaphoreType.DMA((groups, chips - 1)),
        ],
        compiler_params=pltpu.CompilerParams(
            collective_id=1, has_side_effects=True, vmem_limit_bytes=48 << 20
        ),
    )(features, kv_weight, query_rows, grad_rows)


def per_device(queries, encodings, kv_weight, grad_out, neighbour_owner, neighbour_slot):
    seq_count = lax.axis_size("seq")
    seq_index = lax.axis_index("seq")
    token_rows, width = queries.shape
    requests = token_rows // SPAN * NEIGHBOURS
    tile_rows, _, part = encodings.shape
    forward = [(i, (i + 1) % seq_count) for i in range(seq_count)]
    backward = [((i + 1) % seq_count, i) for i in range(seq_count)]

    tile = neighbour_owner * tile_rows + neighbour_slot
    tile = jnp.roll(tile, 1, axis=0).reshape(seq_count, requests)
    tile = lax.dynamic_index_in_dim(tile, seq_index, 0, keepdims=False)

    stored = gather_tiles(encodings, seq_count).reshape(-1, NEIGHBOUR_LEN, part)
    picked = stored[tile].reshape(requests * NEIGHBOUR_LEN, part)
    features = lax.all_gather(picked, "head", axis=0, tiled=False)

    edge = jnp.stack([queries[-1:], grad_out[-1:]], 0)
    edge = lax.ppermute(edge, "seq", forward)
    row = lax.broadcasted_iota(jnp.int32, (token_rows, 1), 0)
    unattending = (seq_index == 0) & (row >= 1) & (row < SPAN)
    zero = jnp.zeros((), BF16)

    def shifted(rows, first):
        rows = jnp.concatenate([first, rows[:-1]], 0)
        return jnp.where(unattending, zero, rows)

    query_rows = shifted(queries, edge[0])
    grad_rows = shifted(grad_out, edge[1])
    att, qgrad, mine = run_groups(features, kv_weight, query_rows, grad_rows)

    att = jnp.where(unattending, zero, att)
    last = lax.ppermute(jnp.stack([att[:1], qgrad[:1]], 0), "seq", backward)
    attended = jnp.concatenate([att[1:], last[0]], 0)
    qgrad = jnp.concatenate([qgrad[1:], last[1]], 0).reshape(-1, SPAN, width)
    query_grad = lax.all_to_all(qgrad, "head", split_axis=1, concat_axis=2, tiled=True)

    mine = mine.reshape(requests, NEIGHBOUR_LEN, part)
    share = (jnp.arange(seq_count * tile_rows)[:, None] == tile[None, :]).astype(F32)
    total = scatter_tiles(share, mine, seq_count, tile_rows)
    return attended, query_grad, total


def solution(mesh):
    in_specs = (
        P("seq", "head"),
        P("seq", None, "head"),
        P(None, None, "head"),
        P("seq", "head"),
        P(),
        P(),
    )
    out_specs = (P("seq", "head"), P("seq", "head", None), P("seq", None, "head"))
    return jax.shard_map(
        per_device, mesh=mesh, in_specs=in_specs, out_specs=out_specs, check_vma=False
    )
```

```python
import functools

import jax
import jax.numpy as jnp
from jax import lax
from jax.experimental import pallas as pl
from jax.experimental.pallas import tpu as pltpu
from jax.sharding import PartitionSpec as P

HEAD_DIM = 128
SPAN = 64
NEIGHBOURS = 2
NEIGHBOUR_LEN = 128
WINDOW = NEIGHBOURS * NEIGHBOUR_LEN
SCALE = HEAD_DIM ** (-0.5)
F32 = jnp.float32
BF16 = jnp.bfloat16


def dot(a, b, da, db):
    return lax.dot_general(a, b, (((da,), (db,)), ((), ())), preferred_element_type=F32)


def ring_place(index, count):
    odd = index % 2
    return (1 - odd) * (index // 2) + odd * (count - 1 - index // 2)


def ring_index(place, count):
    place = (place + 2 * count) % count
    upper = place // (count // 2)
    return (1 - upper) * 2 * place + upper * (2 * (count - 1 - place) + 1)


def meet(others):
    barrier = pltpu.get_barrier_semaphore()
    for axis, other in others:
        pl.semaphore_signal(
            barrier, inc=1, device_id={axis: other}, device_id_type=pl.DeviceIdType.MESH
        )
    pl.semaphore_wait(barrier, len(others))


def remote(src, dst, send, recv, axis, other):
    return pltpu.make_async_remote_copy(
        src_ref=src,
        dst_ref=dst,
        send_sem=send,
        recv_sem=recv,
        device_id={axis: other},
        device_id_type=pl.DeviceIdType.MESH,
    )


def gather_body(
    count, pick_ref, shard_ref, edge_ref, picked_ref, edge_out, stored, send, recv, edge_send, edge_recv
):
    me = lax.axis_index("seq")
    place = ring_place(me, count)
    neighbours = (ring_index(place + 1, count), ring_index(place - 1, count))
    after = (me + 1) % count
    before = (me + count - 1) % count
    meet([("seq", other) for other in neighbours + (after, before)])
    stored[me] = shard_ref[...]
    rows = shard_ref.shape[1] // 2
    hops = ((count // 2, count // 2 - 1), (count // 2 - 1, count // 2))

    def copy(way, half, step):
        owner = ring_index(place - step if way == 0 else place + step, count)
        ref = stored.at[owner, :, pl.ds(half * rows, rows), :]
        return remote(
            ref, ref, send.at[way, half, step], recv.at[way, half, step], "seq", neighbours[way]
        )

    lanes = [(way, half) for half in range(2) for way in range(2)]
    edge = remote(edge_ref, edge_out, edge_send.at[0], edge_recv.at[0], "seq", after)
    for step in range(count // 2):
        for way, half in lanes:
            if step < hops[way][half]:
                if step > 0:
                    copy(way, half, step - 1).wait_recv()
                copy(way, half, step).start()
        if step == 0:
            edge.start()
    for way, half in lanes:
        copy(way, half, hops[way][half] - 1).wait_recv()
    for r in range(picked_ref.shape[0]):
        picked_ref[r] = stored[pick_ref[0, r], pick_ref[1, r]]
    edge.wait()
    for way, half in lanes:
        for step in range(hops[way][half]):
            copy(way, half, step).wait_send()


def gather_tiles(pick, shard, edge, count):
    tiles, rows, part = shard.shape
    vmem = pl.BlockSpec(memory_space=pltpu.VMEM)
    return pl.pallas_call(
        functools.partial(gather_body, count),
        in_specs=[pl.BlockSpec(memory_space=pltpu.SMEM), vmem, vmem],
        out_specs=[vmem, vmem],
        out_shape=[
            jax.ShapeDtypeStruct((pick.shape[1], rows, part), shard.dtype),
            jax.ShapeDtypeStruct(edge.shape, edge.dtype),
        ],
        scratch_shapes=[
            pltpu.VMEM((count, tiles, rows, part), shard.dtype),
            pltpu.SemaphoreType.DMA((2, 2, count // 2)),
            pltpu.SemaphoreType.DMA((2, 2, count // 2)),
            pltpu.SemaphoreType.DMA((1,)),
            pltpu.SemaphoreType.DMA((1,)),
        ],
        compiler_params=pltpu.CompilerParams(
            collective_id=0, has_side_effects=True, vmem_limit_bytes=32 << 20
        ),
    )(pick, shard, edge)


def scatter_body(count, share_ref, mine_ref, out_ref, buf, send, recv):
    me = lax.axis_index("seq")
    place = ring_place(me, count)
    neighbours = (ring_index(place + 1, count), ring_index(place - 1, count))
    meet([("seq", other) for other in neighbours])
    tiles, length, _ = out_ref.shape
    requests = mine_ref.shape[0]
    rows = length // 2

    def own(way, target, k):
        total = None
        for r in range(requests):
            piece = share_ref[target * tiles + k, r] * mine_ref[r, way * rows : (way + 1) * rows, :]
            total = piece if total is None else total + piece
        return total

    def target_of(way, step):
        return ring_index(place - 1 - step if way == 0 else place + 1 + step, count)

    def copy(way, step, k):
        return remote(
            buf.at[way, step, k],
            buf.at[way, step + 1, k],
            send.at[way, step, k],
            recv.at[way, step, k],
            "seq",
            neighbours[way],
        )

    for k in range(tiles):
        for way in range(2):
            buf[way, 0, k] = own(way, target_of(way, 0), k)
            copy(way, 0, k).start()

    def step_body(step, carry):
        for k in range(tiles):
            for way in range(2):
                piece = own(way, target_of(way, step), k)
                copy(way, step - 1, k).wait_recv()
                buf[way, step, k] = buf[way, step, k] + piece
                copy(way, step, k).start()
        return carry

    lax.fori_loop(1, count - 1, step_body, 0)
    for k in range(tiles):
        for way in range(2):
            piece = own(way, me, k)
            copy(way, count - 2, k).wait_recv()
            out_ref[k, way * rows : (way + 1) * rows, :] = (buf[way, count - 1, k] + piece).astype(
                out_ref.dtype
            )

    def drain(step, carry):
        for k in range(tiles):
            for way in range(2):
                copy(way, step, k).wait_send()
        return carry

    lax.fori_loop(0, count - 1, drain, 0)


def scatter_tiles(share, mine, count, tiles):
    _, length, part = mine.shape
    return pl.pallas_call(
        functools.partial(scatter_body, count),
        in_specs=[
            pl.BlockSpec(memory_space=pltpu.SMEM),
            pl.BlockSpec(memory_space=pltpu.VMEM),
        ],
        out_specs=pl.BlockSpec(memory_space=pltpu.VMEM),
        out_shape=jax.ShapeDtypeStruct((tiles, length, part), BF16),
        scratch_shapes=[
            pltpu.VMEM((2, count, tiles, length // 2, part), F32),
            pltpu.SemaphoreType.DMA((2, count - 1, tiles)),
            pltpu.SemaphoreType.DMA((2, count - 1, tiles)),
        ],
        compiler_params=pltpu.CompilerParams(
            collective_id=2, has_side_effects=True, vmem_limit_bytes=32 << 20
        ),
    )(share, mine)


def group_body(
    parts, count, picked_ref, weight_ref, query_ref, grad_ref, edge_ref,
    att_ref, qgrad_ref, out_ref,
    feat, kv, kv_grad, rows_in, tail, att_rows, qgrad_rows, edge_out, edge_in, qout, qin,
    term, from_core, across, from_chip,
    pick_send, pick_recv, far_send, far_recv, pass_send, pass_recv,
    edge_send, edge_recv, q_send, q_recv, core_send, core_recv, chip_send, chip_recv,
):
    head = lax.axis_index("head")
    seq = lax.axis_index("seq")
    core, chip = head % 2, head // 2
    chips = parts // 2
    sibling = chip * 2 + 1 - core
    peers = [((chip + d) % chips) * 2 + core for d in range(1, chips)]
    others = [(head + d) % parts for d in range(1, parts)]
    before = (seq + count - 1) % count
    after = (seq + 1) % count
    meet([("head", other) for other in others] + [("seq", before), ("seq", after)])
    part = picked_ref.shape[2]
    width = query_ref.shape[1]
    groups = query_ref.shape[0] // SPAN
    segment = SPAN // parts

    def to_sibling(i):
        return remote(
            picked_ref.at[i], feat.at[head, i], pick_send.at[i], pick_recv.at[i], "head", sibling
        )

    def to_far(i, d):
        return remote(
            picked_ref.at[i],
            feat.at[head, i],
            far_send.at[i, d - 1],
            far_recv.at[i, d - 1],
            "head",
            peers[d - 1],
        )

    def pass_far(i, d):
        ref = feat.at[((chip + chips - d) % chips) * 2 + core, i]
        return remote(
            ref, ref, pass_send.at[i, d - 1], pass_recv.at[i, d - 1], "head", sibling
        )

    def hand_over(i):
        for d in range(1, chips):
            to_far(i, d).wait_recv()
            pass_far(i, d).start()

    def to_core(i):
        return remote(
            term.at[i, 1 - core], from_core.at[i], core_send.at[i], core_recv.at[i], "head", sibling
        )

    def to_chip(i, d):
        return remote(
            across.at[i, d - 1],
            from_chip.at[i, d - 1],
            chip_send.at[i, d - 1],
            chip_recv.at[i, d - 1],
            "head",
            peers[d - 1],
        )

    def to_head(i, d):
        return remote(
            qout.at[i, others[d - 1]],
            qin.at[head, i],
            q_send.at[i, d - 1],
            q_recv.at[i, d - 1],
            "head",
            others[d - 1],
        )

    edge = remote(edge_out, edge_in, edge_send.at[0], edge_recv.at[0], "seq", before)

    def pass_on(i):
        to_core(i).wait_recv()
        for d in range(1, chips):
            target = (chip + d) % chips
            across[i, d - 1] = term[i, core, target] + from_core[i, target]
            to_chip(i, d).start()

    last16 = lax.broadcasted_iota(jnp.int32, (16, width), 0) == 15
    last_segment = lax.broadcasted_iota(jnp.int32, (segment, width), 0) == segment - 1
    place = lax.broadcasted_iota(jnp.int32, (SPAN, width), 0)

    def finish_span(i, att16, qgrad16):
        rows = pl.ds(pl.multiple_of(i * SPAN + SPAN - 16, 16), 16)
        att_ref[rows, :] = jnp.where(last16, att16, att_ref[rows, :].astype(F32)).astype(BF16)
        qout[i, parts - 1] = jnp.where(
            last_segment, qgrad16[16 - segment :], qout[i, parts - 1].astype(F32)
        ).astype(BF16)
        qin[head, i] = qout[i, head]
        for d in range(1, parts):
            to_head(i, d).start()

    for i in range(groups):
        for d in range(1, chips):
            to_far(i, d).start()
        to_sibling(i).start()
    for i in range(groups):
        feat[head, i] = picked_ref[i]
    tail[...] = edge_ref[...]
    hand_over(0)

    def group(i, carry):
        tokens = pl.ds(pl.multiple_of(i * SPAN, SPAN), SPAN)
        limit = jnp.where(jnp.logical_and(seq == 0, i == 0), SPAN - 1, 0)
        for c, ref in ((0, query_ref), (1, grad_ref)):
            rows = ref[tokens, :].astype(F32)
            ending = jnp.where(last16, tail[c].astype(F32), rows[SPAN - 16 :])
            tail[c] = rows[SPAN - 16 :].astype(BF16)
            rows = jnp.concatenate([rows[: SPAN - 16], ending], 0)
            rows_in[c] = jnp.where(place >= limit, rows, 0.0).astype(BF16)
        to_sibling(i).wait_recv()
        for d in range(1, chips):
            pass_far(i, d).wait_recv()
        for c in range(2):
            total = None
            for j in range(parts):
                piece = dot(feat[j, i], weight_ref[c, j * part : (j + 1) * part, :], 1, 0)
                total = piece if total is None else total + piece
            kv[c] = total.astype(BF16)

        @pl.when(i + 1 < groups)
        def _():
            hand_over(i + 1)

        for h in range(width // HEAD_DIM):
            cols = slice(h * HEAD_DIM, (h + 1) * HEAD_DIM)
            q = rows_in[0, :, cols]
            g = rows_in[1, :, cols]
            k = kv[0, :, cols]
            v = kv[1, :, cols]
            scores = dot(q, k, 1, 1) * SCALE
            dprob = dot(g, v, 1, 1)
            expo = jnp.exp(scores - jnp.max(scores, axis=-1, keepdims=True))
            probs = expo / jnp.sum(expo, axis=-1, keepdims=True)
            half = probs.astype(BF16)
            delta = jnp.sum(probs * dprob, axis=-1, keepdims=True)
            dscore = (probs * (dprob - delta)).astype(BF16)
            att_rows[:, cols] = dot(half, v, 1, 0)
            qgrad_rows[:, cols] = dot(dscore, k, 1, 0) * SCALE
            kv_grad[0, :, cols] = (dot(dscore, q, 0, 0) * SCALE).astype(BF16)
            kv_grad[1, :, cols] = dot(half, g, 0, 0).astype(BF16)
        for j in range(parts):
            rows = slice(j * part, (j + 1) * part)
            term[i, j % 2, j // 2] = dot(kv_grad[0], weight_ref[0, rows, :], 1, 1) + dot(
                kv_grad[1], weight_ref[1, rows, :], 1, 1
            )
        to_core(i).start()
        att = jnp.where(place >= limit, att_rows[...], 0.0)
        att_ref[tokens, :] = att.astype(BF16)
        for j in range(parts):
            qout[i, j] = qgrad_rows[j * segment : (j + 1) * segment, :].astype(BF16)

        @pl.when(i == 0)
        def _():
            edge_out[0] = att_rows[SPAN - 16 :, :].astype(BF16)
            edge_out[1] = qgrad_rows[SPAN - 16 :, :].astype(BF16)
            edge.start()

        @pl.when(i > 0)
        def _():
            pass_on(i - 1)
            finish_span(i - 1, att_rows[SPAN - 16 :, :], qgrad_rows[SPAN - 16 :, :])

        return carry

    lax.fori_loop(0, groups, group, 0)
    pass_on(groups - 1)
    edge.wait_recv()
    finish_span(groups - 1, edge_in[0].astype(F32), edge_in[1].astype(F32))
    for i in range(groups):
        total = term[i, core, chip] + from_core[i, chip]
        for d in range(1, chips):
            to_chip(i, d).wait_recv()
            total = total + from_chip[i, d - 1]
        out_ref[i * WINDOW : (i + 1) * WINDOW, :] = total
    edge.wait_send()
    for i in range(groups):
        for d in range(1, parts):
            to_head(i, d).wait_recv()
        for j in range(parts):
            qgrad_ref[i, :, j * width : (j + 1) * width] = qin[j, i]
    for i in range(groups):
        to_core(i).wait_send()
        to_sibling(i).wait_send()
        for d in range(1, chips):
            to_chip(i, d).wait_send()
            to_far(i, d).wait_send()
            pass_far(i, d).wait_send()
        for d in range(1, parts):
            to_head(i, d).wait_send()


def run_groups(picked, kv_weight, queries, grad_out, edge, parts, count):
    groups, rows, part = picked.shape
    token_rows, width = queries.shape
    chips = parts // 2
    segment = SPAN // parts
    vmem = pl.BlockSpec(memory_space=pltpu.VMEM)
    dma = pltpu.SemaphoreType.DMA
    return pl.pallas_call(
        functools.partial(group_body, parts, count),
        in_specs=[vmem] * 5,
        out_specs=[vmem] * 3,
        out_shape=[
            jax.ShapeDtypeStruct((token_rows, width), BF16),
            jax.ShapeDtypeStruct((groups, segment, width * parts), BF16),
            jax.ShapeDtypeStruct((groups * WINDOW, part), F32),
        ],
        scratch_shapes=[
            pltpu.VMEM((parts, groups, WINDOW, part), BF16),
            pltpu.VMEM((2, WINDOW, width), BF16),
            pltpu.VMEM((2, WINDOW, width), BF16),
            pltpu.VMEM((2, SPAN, width), BF16),
            pltpu.VMEM((2, 16, width), BF16),
            pltpu.VMEM((SPAN, width), F32),
            pltpu.VMEM((SPAN, width), F32),
            pltpu.VMEM((2, 16, width), BF16),
            pltpu.VMEM((2, 16, width), BF16),
            pltpu.VMEM((groups, parts, segment, width), BF16),
            pltpu.VMEM((parts, groups, segment, width), BF16),
            pltpu.VMEM((groups, 2, chips, WINDOW, part), F32),
            pltpu.VMEM((groups, chips, WINDOW, part), F32),
            pltpu.VMEM((groups, chips - 1, WINDOW, part), F32),
            pltpu.VMEM((groups, chips - 1, WINDOW, part), F32),
            dma((groups,)),
            dma((groups,)),
            dma((groups, chips - 1)),
            dma((groups, chips - 1)),
            dma((groups, chips - 1)),
            dma((groups, chips - 1)),
            dma((1,)),
            dma((1,)),
            dma((groups, parts - 1)),
            dma((groups, parts - 1)),
            dma((groups,)),
            dma((groups,)),
            dma((groups, chips - 1)),
            dma((groups, chips - 1)),
        ],
        compiler_params=pltpu.CompilerParams(
            collective_id=1, has_side_effects=True, vmem_limit_bytes=48 << 20
        ),
    )(picked, kv_weight, queries, grad_out, edge)


def per_device(queries, encodings, kv_weight, grad_out, neighbour_owner, neighbour_slot):
    seq_count = lax.axis_size("seq")
    seq_index = lax.axis_index("seq")
    parts = lax.axis_size("head")
    token_rows, width = queries.shape
    requests = token_rows // SPAN * NEIGHBOURS
    tile_rows, _, part = encodings.shape

    pick = jnp.stack([neighbour_owner, neighbour_slot], 0)
    pick = jnp.roll(pick, 1, axis=1).reshape(2, seq_count, requests)
    pick = lax.dynamic_index_in_dim(pick, seq_index, 1, keepdims=False)
    edge = jnp.stack([queries[-16:], grad_out[-16:]], 0)
    picked, edge = gather_tiles(pick, encodings, edge, seq_count)
    picked = picked.reshape(requests // NEIGHBOURS, WINDOW, part)
    attended, query_grad, mine = run_groups(
        picked, kv_weight, queries, grad_out, edge, parts, seq_count
    )
    mine = mine.reshape(requests, NEIGHBOUR_LEN, part)
    tile = pick[0] * tile_rows + pick[1]
    share = (jnp.arange(seq_count * tile_rows)[:, None] == tile[None, :]).astype(F32)
    total = scatter_tiles(share, mine, seq_count, tile_rows)
    return attended, query_grad, total


def solution(mesh):
    in_specs = (
        P("seq", "head"),
        P("seq", None, "head"),
        P(None, None, "head"),
        P("seq", "head"),
        P(),
        P(),
    )
    out_specs = (P("seq", "head"), P("seq", "head", None), P("seq", None, "head"))
    return jax.shard_map(
        per_device, mesh=mesh, in_specs=in_specs, out_specs=out_specs, check_vma=False
    )
```

```python
import functools

import jax
import jax.numpy as jnp
from jax import lax
from jax.experimental import pallas as pl
from jax.experimental.pallas import tpu as pltpu
from jax.sharding import PartitionSpec as P

HEAD_DIM = 128
SPAN = 64
NEIGHBOURS = 2
NEIGHBOUR_LEN = 128
WINDOW = NEIGHBOURS * NEIGHBOUR_LEN
SCALE = HEAD_DIM ** (-0.5)
F32 = jnp.float32
BF16 = jnp.bfloat16


def dot(a, b, da, db):
    return lax.dot_general(a, b, (((da,), (db,)), ((), ())), preferred_element_type=F32)


def ring_place(index, count):
    odd = index % 2
    return (1 - odd) * (index // 2) + odd * (count - 1 - index // 2)


def ring_index(place, count):
    place = (place + 2 * count) % count
    upper = place // (count // 2)
    return (1 - upper) * 2 * place + upper * (2 * (count - 1 - place) + 1)


def meet(others):
    barrier = pltpu.get_barrier_semaphore()
    for axis, other in others:
        pl.semaphore_signal(
            barrier, inc=1, device_id={axis: other}, device_id_type=pl.DeviceIdType.MESH
        )
    pl.semaphore_wait(barrier, len(others))


def remote(src, dst, send, recv, axis, other):
    return pltpu.make_async_remote_copy(
        src_ref=src,
        dst_ref=dst,
        send_sem=send,
        recv_sem=recv,
        device_id={axis: other},
        device_id_type=pl.DeviceIdType.MESH,
    )


def gather_body(
    count, pick_ref, shard_ref, query_ref, grad_ref, picked_ref, edge_out, stored,
    send, recv, edge_send, edge_recv,
):
    me = lax.axis_index("seq")
    place = ring_place(me, count)
    neighbours = (ring_index(place + 1, count), ring_index(place - 1, count))
    after = (me + 1) % count
    before = (me + count - 1) % count
    meet([("seq", other) for other in neighbours + (after, before)])
    stored[me] = shard_ref[...]
    rows = shard_ref.shape[1] // 2
    hops = ((count // 2, count // 2 - 1), (count // 2 - 1, count // 2))

    def copy(way, half, step):
        owner = ring_index(place - step if way == 0 else place + step, count)
        ref = stored.at[owner, :, pl.ds(half * rows, rows), :]
        return remote(
            ref, ref, send.at[way, half, step], recv.at[way, half, step], "seq", neighbours[way]
        )

    lanes = [(way, half) for half in range(2) for way in range(2)]
    ending = pl.ds(query_ref.shape[0] - 16, 16)
    edges = [
        remote(ref.at[ending, :], edge_out.at[c], edge_send.at[c], edge_recv.at[c], "seq", after)
        for c, ref in ((0, query_ref), (1, grad_ref))
    ]
    for step in range(count // 2):
        for way, half in lanes:
            if step < hops[way][half]:
                if step > 0:
                    copy(way, half, step - 1).wait_recv()
                copy(way, half, step).start()
        if step == 0:
            for edge in edges:
                edge.start()
    for way, half in lanes:
        copy(way, half, hops[way][half] - 1).wait_recv()
    for r in range(picked_ref.shape[0]):
        picked_ref[r] = stored[pick_ref[0, r], pick_ref[1, r]]
    for edge in edges:
        edge.wait()
    for way, half in lanes:
        for step in range(hops[way][half]):
            copy(way, half, step).wait_send()


def gather_tiles(pick, shard, queries, grad_out, count):
    tiles, rows, part = shard.shape
    vmem = pl.BlockSpec(memory_space=pltpu.VMEM)
    return pl.pallas_call(
        functools.partial(gather_body, count),
        in_specs=[pl.BlockSpec(memory_space=pltpu.SMEM), vmem]
        + [pl.BlockSpec(memory_space=pl.ANY)] * 2,
        out_specs=[vmem, vmem],
        out_shape=[
            jax.ShapeDtypeStruct((pick.shape[1], rows, part), shard.dtype),
            jax.ShapeDtypeStruct((2, 16, queries.shape[1]), queries.dtype),
        ],
        scratch_shapes=[
            pltpu.VMEM((count, tiles, rows, part), shard.dtype),
            pltpu.SemaphoreType.DMA((2, 2, count // 2)),
            pltpu.SemaphoreType.DMA((2, 2, count // 2)),
            pltpu.SemaphoreType.DMA((2,)),
            pltpu.SemaphoreType.DMA((2,)),
        ],
        compiler_params=pltpu.CompilerParams(
            collective_id=0, has_side_effects=True, vmem_limit_bytes=32 << 20
        ),
    )(pick, shard, queries, grad_out)


def scatter_body(
    count, share_ref, mine_ref, qout, out_ref, qgrad_ref, buf, qin, send, recv, q_send, q_recv
):
    head = lax.axis_index("head")
    groups, parts, _, width = qout.shape
    others = [(head + d) % parts for d in range(1, parts)]
    me = lax.axis_index("seq")
    place = ring_place(me, count)
    neighbours = (ring_index(place + 1, count), ring_index(place - 1, count))
    meet([("seq", other) for other in neighbours] + [("head", other) for other in others])
    tiles, length, _ = out_ref.shape
    requests = mine_ref.shape[0]
    rows = length // 2

    def own(way, target, k):
        total = None
        for r in range(requests):
            piece = share_ref[target * tiles + k, r] * mine_ref[r, way * rows : (way + 1) * rows, :]
            total = piece if total is None else total + piece
        return total

    def target_of(way, step):
        return ring_index(place - 1 - step if way == 0 else place + 1 + step, count)

    def copy(way, step, k):
        return remote(
            buf.at[way, step, k],
            buf.at[way, step + 1, k],
            send.at[way, step, k],
            recv.at[way, step, k],
            "seq",
            neighbours[way],
        )

    def to_head(i, d):
        return remote(
            qout.at[i, others[d - 1]],
            qin.at[head, i],
            q_send.at[i, d - 1],
            q_recv.at[i, d - 1],
            "head",
            others[d - 1],
        )

    for k in range(tiles):
        for way in range(2):
            buf[way, 0, k] = own(way, target_of(way, 0), k)
            copy(way, 0, k).start()

    for i in range(groups):
        for d in range(1, parts):
            to_head(i, d).start()
        qgrad_ref[i, :, pl.ds(pl.multiple_of(head * width, width), width)] = qout[i, head]

    def step_body(step, carry):
        for k in range(tiles):
            for way in range(2):
                piece = own(way, target_of(way, step), k)
                copy(way, step - 1, k).wait_recv()
                buf[way, step, k] = buf[way, step, k] + piece
                copy(way, step, k).start()
        return carry

    lax.fori_loop(1, count - 1, step_body, 0)
    for i in range(groups):
        for d in range(1, parts):
            source = (head + parts - d) % parts
            to_head(i, d).wait_recv()
            columns = pl.ds(pl.multiple_of(source * width, width), width)
            qgrad_ref[i, :, columns] = qin[source, i]
    for k in range(tiles):
        for way in range(2):
            piece = own(way, me, k)
            copy(way, count - 2, k).wait_recv()
            out_ref[k, way * rows : (way + 1) * rows, :] = (buf[way, count - 1, k] + piece).astype(
                out_ref.dtype
            )

    def drain(step, carry):
        for k in range(tiles):
            for way in range(2):
                copy(way, step, k).wait_send()
        return carry

    lax.fori_loop(0, count - 1, drain, 0)
    for i in range(groups):
        for d in range(1, parts):
            to_head(i, d).wait_send()


def scatter_tiles(share, mine, qout, count, tiles):
    _, length, part = mine.shape
    groups, parts, segment, width = qout.shape
    vmem = pl.BlockSpec(memory_space=pltpu.VMEM)
    return pl.pallas_call(
        functools.partial(scatter_body, count),
        in_specs=[
            pl.BlockSpec(memory_space=pltpu.SMEM),
            vmem,
            vmem,
        ],
        out_specs=[vmem, vmem],
        out_shape=[
            jax.ShapeDtypeStruct((tiles, length, part), BF16),
            jax.ShapeDtypeStruct((groups, segment, parts * width), BF16),
        ],
        scratch_shapes=[
            pltpu.VMEM((2, count, tiles, length // 2, part), F32),
            pltpu.VMEM((parts, groups, segment, width), BF16),
            pltpu.SemaphoreType.DMA((2, count - 1, tiles)),
            pltpu.SemaphoreType.DMA((2, count - 1, tiles)),
            pltpu.SemaphoreType.DMA((groups, parts - 1)),
            pltpu.SemaphoreType.DMA((groups, parts - 1)),
        ],
        compiler_params=pltpu.CompilerParams(
            collective_id=2, has_side_effects=True, vmem_limit_bytes=32 << 20
        ),
    )(share, mine, qout)


def group_body(
    parts, count, picked_ref, weight_ref, query_ref, grad_ref, edge_ref,
    att_ref, qout, out_ref,
    feat, kv, kv_grad, rows_in, tail, att_rows, qgrad_rows, edge_out, edge_in,
    term, from_core, across, from_chip,
    pick_send, pick_recv, far_send, far_recv, pass_send, pass_recv,
    edge_send, edge_recv, core_send, core_recv, chip_send, chip_recv,
):
    head = lax.axis_index("head")
    seq = lax.axis_index("seq")
    core, chip = head % 2, head // 2
    chips = parts // 2
    sibling = chip * 2 + 1 - core
    peers = [((chip + d) % chips) * 2 + core for d in range(1, chips)]
    before = (seq + count - 1) % count
    after = (seq + 1) % count
    meet([("head", other) for other in [sibling] + peers] + [("seq", before), ("seq", after)])
    part = picked_ref.shape[2]
    width = query_ref.shape[1]
    groups = query_ref.shape[0] // SPAN
    segment = SPAN // parts

    def to_sibling(i):
        return remote(
            picked_ref.at[i], feat.at[head, i], pick_send.at[i], pick_recv.at[i], "head", sibling
        )

    def to_far(i, d):
        return remote(
            picked_ref.at[i],
            feat.at[head, i],
            far_send.at[i, d - 1],
            far_recv.at[i, d - 1],
            "head",
            peers[d - 1],
        )

    def pass_far(i, d):
        ref = feat.at[((chip + chips - d) % chips) * 2 + core, i]
        return remote(
            ref, ref, pass_send.at[i, d - 1], pass_recv.at[i, d - 1], "head", sibling
        )

    def hand_over(i):
        for d in range(1, chips):
            to_far(i, d).wait_recv()
            pass_far(i, d).start()

    def to_core(i, d):
        target = (chip + d) % chips
        return remote(
            term.at[i, 1 - core, target],
            from_core.at[i, target],
            core_send.at[i, d],
            core_recv.at[i, d],
            "head",
            sibling,
        )

    def to_chip(i, d):
        return remote(
            across.at[i, d - 1],
            from_chip.at[i, d - 1],
            chip_send.at[i, d - 1],
            chip_recv.at[i, d - 1],
            "head",
            peers[d - 1],
        )

    edge = remote(edge_out, edge_in, edge_send.at[0], edge_recv.at[0], "seq", before)

    def pass_on(i):
        for d in range(1, chips):
            target = (chip + d) % chips
            to_core(i, d).wait_recv()
            across[i, d - 1] = term[i, core, target] + from_core[i, target]
            to_chip(i, d).start()

    last16 = lax.broadcasted_iota(jnp.int32, (16, width), 0) == 15
    last_segment = lax.broadcasted_iota(jnp.int32, (segment, width), 0) == segment - 1
    place = lax.broadcasted_iota(jnp.int32, (SPAN, width), 0)

    def finish_span(i, att16, qgrad16):
        rows = pl.ds(pl.multiple_of(i * SPAN + SPAN - 16, 16), 16)
        att_ref[rows, :] = jnp.where(last16, att16, att_ref[rows, :].astype(F32)).astype(BF16)
        qout[i, parts - 1] = jnp.where(
            last_segment, qgrad16[16 - segment :], qout[i, parts - 1].astype(F32)
        ).astype(BF16)

    for i in range(groups):
        for d in range(1, chips):
            to_far(i, d).start()
        to_sibling(i).start()
    for i in range(groups):
        feat[head, i] = picked_ref[i]
    tail[...] = edge_ref[...]
    hand_over(0)

    def group(i, carry):
        tokens = pl.ds(pl.multiple_of(i * SPAN, SPAN), SPAN)
        limit = jnp.where(jnp.logical_and(seq == 0, i == 0), SPAN - 1, 0)
        for c, ref in ((0, query_ref), (1, grad_ref)):
            rows = ref[tokens, :].astype(F32)
            ending = jnp.where(last16, tail[c].astype(F32), rows[SPAN - 16 :])
            tail[c] = rows[SPAN - 16 :].astype(BF16)
            rows = jnp.concatenate([rows[: SPAN - 16], ending], 0)
            rows_in[c] = jnp.where(place >= limit, rows, 0.0).astype(BF16)
        to_sibling(i).wait_recv()
        for d in range(1, chips):
            pass_far(i, d).wait_recv()
        for c in range(2):
            total = None
            for j in range(parts):
                piece = dot(feat[j, i], weight_ref[c, j * part : (j + 1) * part, :], 1, 0)
                total = piece if total is None else total + piece
            kv[c] = total.astype(BF16)

        @pl.when(i + 1 < groups)
        def _():
            hand_over(i + 1)

        for h in range(width // HEAD_DIM):
            cols = slice(h * HEAD_DIM, (h + 1) * HEAD_DIM)
            q = rows_in[0, :, cols]
            g = rows_in[1, :, cols]
            k = kv[0, :, cols]
            v = kv[1, :, cols]
            scores = dot(q, k, 1, 1) * SCALE
            dprob = dot(g, v, 1, 1)
            expo = jnp.exp(scores - jnp.max(scores, axis=-1, keepdims=True))
            probs = expo / jnp.sum(expo, axis=-1, keepdims=True)
            half = probs.astype(BF16)
            delta = jnp.sum(probs * dprob, axis=-1, keepdims=True)
            dscore = (probs * (dprob - delta)).astype(BF16)
            att_rows[:, cols] = dot(half, v, 1, 0)
            qgrad_rows[:, cols] = dot(dscore, k, 1, 0) * SCALE
            kv_grad[0, :, cols] = (dot(dscore, q, 0, 0) * SCALE).astype(BF16)
            kv_grad[1, :, cols] = dot(half, g, 0, 0).astype(BF16)
        for d in [*range(1, chips), 0]:
            target = (chip + d) % chips
            for c in (1 - core, core):
                first = (target * 2 + c) * part
                rows = pl.ds(pl.multiple_of(first, part), part)
                term[i, c, target] = dot(kv_grad[0], weight_ref[0, rows, :], 1, 1) + dot(
                    kv_grad[1], weight_ref[1, rows, :], 1, 1
                )
                if c is not core:
                    to_core(i, d).start()
        att = jnp.where(place >= limit, att_rows[...], 0.0)
        att_ref[tokens, :] = att.astype(BF16)
        for j in range(parts):
            qout[i, j] = qgrad_rows[j * segment : (j + 1) * segment, :].astype(BF16)

        @pl.when(i == 0)
        def _():
            edge_out[0] = att_rows[SPAN - 16 :, :].astype(BF16)
            edge_out[1] = qgrad_rows[SPAN - 16 :, :].astype(BF16)
            edge.start()

        @pl.when(i > 0)
        def _():
            finish_span(i - 1, att_rows[SPAN - 16 :, :], qgrad_rows[SPAN - 16 :, :])

        pass_on(i)
        return carry

    lax.fori_loop(0, groups, group, 0)
    edge.wait_recv()
    finish_span(groups - 1, edge_in[0].astype(F32), edge_in[1].astype(F32))
    for i in range(groups):
        to_core(i, 0).wait_recv()
        total = term[i, core, chip] + from_core[i, chip]
        for d in range(1, chips):
            to_chip(i, d).wait_recv()
            total = total + from_chip[i, d - 1]
        out_ref[i * WINDOW : (i + 1) * WINDOW, :] = total
    edge.wait_send()
    for i in range(groups):
        for d in range(chips):
            to_core(i, d).wait_send()
        to_sibling(i).wait_send()
        for d in range(1, chips):
            to_chip(i, d).wait_send()
            to_far(i, d).wait_send()
            pass_far(i, d).wait_send()


def run_groups(picked, kv_weight, queries, grad_out, edge, parts, count):
    groups, rows, part = picked.shape
    token_rows, width = queries.shape
    chips = parts // 2
    segment = SPAN // parts
    vmem = pl.BlockSpec(memory_space=pltpu.VMEM)
    dma = pltpu.SemaphoreType.DMA
    return pl.pallas_call(
        functools.partial(group_body, parts, count),
        in_specs=[vmem] * 5,
        out_specs=[vmem] * 3,
        out_shape=[
            jax.ShapeDtypeStruct((token_rows, width), BF16),
            jax.ShapeDtypeStruct((groups, parts, segment, width), BF16),
            jax.ShapeDtypeStruct((groups * WINDOW, part), F32),
        ],
        scratch_shapes=[
            pltpu.VMEM((parts, groups, WINDOW, part), BF16),
            pltpu.VMEM((2, WINDOW, width), BF16),
            pltpu.VMEM((2, WINDOW, width), BF16),
            pltpu.VMEM((2, SPAN, width), BF16),
            pltpu.VMEM((2, 16, width), BF16),
            pltpu.VMEM((SPAN, width), F32),
            pltpu.VMEM((SPAN, width), F32),
            pltpu.VMEM((2, 16, width), BF16),
            pltpu.VMEM((2, 16, width), BF16),
            pltpu.VMEM((groups, 2, chips, WINDOW, part), F32),
            pltpu.VMEM((groups, chips, WINDOW, part), F32),
            pltpu.VMEM((groups, chips - 1, WINDOW, part), F32),
            pltpu.VMEM((groups, chips - 1, WINDOW, part), F32),
            dma((groups,)),
            dma((groups,)),
            dma((groups, chips - 1)),
            dma((groups, chips - 1)),
            dma((groups, chips - 1)),
            dma((groups, chips - 1)),
            dma((1,)),
            dma((1,)),
            dma((groups, chips)),
            dma((groups, chips)),
            dma((groups, chips - 1)),
            dma((groups, chips - 1)),
        ],
        compiler_params=pltpu.CompilerParams(
            collective_id=1, has_side_effects=True, vmem_limit_bytes=48 << 20
        ),
    )(picked, kv_weight, queries, grad_out, edge)


def per_device(queries, encodings, kv_weight, grad_out, neighbour_owner, neighbour_slot):
    seq_count = lax.axis_size("seq")
    seq_index = lax.axis_index("seq")
    parts = lax.axis_size("head")
    token_rows, width = queries.shape
    requests = token_rows // SPAN * NEIGHBOURS
    tile_rows, _, part = encodings.shape

    pick = jnp.stack([neighbour_owner, neighbour_slot], 0)
    pick = jnp.roll(pick, 1, axis=1).reshape(2, seq_count, requests)
    pick = lax.dynamic_index_in_dim(pick, seq_index, 1, keepdims=False)
    picked, edge = gather_tiles(pick, encodings, queries, grad_out, seq_count)
    picked = picked.reshape(requests // NEIGHBOURS, WINDOW, part)
    attended, qout, mine = run_groups(
        picked, kv_weight, queries, grad_out, edge, parts, seq_count
    )
    mine = mine.reshape(requests, NEIGHBOUR_LEN, part)
    tile = pick[0] * tile_rows + pick[1]
    share = (jnp.arange(seq_count * tile_rows)[:, None] == tile[None, :]).astype(F32)
    total, query_grad = scatter_tiles(share, mine, qout, seq_count, tile_rows)
    return attended, query_grad, total


def solution(mesh):
    in_specs = (
        P("seq", "head"),
        P("seq", None, "head"),
        P(None, None, "head"),
        P("seq", "head"),
        P(),
        P(),
    )
    out_specs = (P("seq", "head"), P("seq", "head", None), P("seq", None, "head"))
    return jax.shard_map(
        per_device, mesh=mesh, in_specs=in_specs, out_specs=out_specs, check_vma=False
    )
```

```python
import functools

import jax
import jax.numpy as jnp
from jax import lax
from jax.experimental import pallas as pl
from jax.experimental.pallas import tpu as pltpu
from jax.sharding import PartitionSpec as P

HEAD_DIM = 128
SPAN = 64
NEIGHBOURS = 2
NEIGHBOUR_LEN = 128
WINDOW = NEIGHBOURS * NEIGHBOUR_LEN
SCALE = HEAD_DIM ** (-0.5)
F32 = jnp.float32
BF16 = jnp.bfloat16


def dot(a, b, da, db):
    return lax.dot_general(a, b, (((da,), (db,)), ((), ())), preferred_element_type=F32)


def ring_place(index, count):
    odd = index % 2
    return (1 - odd) * (index // 2) + odd * (count - 1 - index // 2)


def ring_index(place, count):
    place = (place + 2 * count) % count
    upper = place // (count // 2)
    return (1 - upper) * 2 * place + upper * (2 * (count - 1 - place) + 1)


def meet(others):
    barrier = pltpu.get_barrier_semaphore()
    for axis, other in others:
        pl.semaphore_signal(
            barrier, inc=1, device_id={axis: other}, device_id_type=pl.DeviceIdType.MESH
        )
    pl.semaphore_wait(barrier, len(others))


def remote(src, dst, send, recv, axis, other):
    return pltpu.make_async_remote_copy(
        src_ref=src,
        dst_ref=dst,
        send_sem=send,
        recv_sem=recv,
        device_id={axis: other},
        device_id_type=pl.DeviceIdType.MESH,
    )


def gather_body(
    count, pick_ref, shard_ref, query_ref, grad_ref, picked_ref, edge_out, stored,
    send, recv, edge_send, edge_recv,
):
    me = lax.axis_index("seq")
    place = ring_place(me, count)
    neighbours = (ring_index(place + 1, count), ring_index(place - 1, count))
    after = (me + 1) % count
    before = (me + count - 1) % count
    meet([("seq", other) for other in neighbours + (after, before)])
    stored[me] = shard_ref[...]
    rows = shard_ref.shape[1] // 2
    hops = ((count // 2, count // 2 - 1), (count // 2 - 1, count // 2))

    def copy(way, half, step):
        owner = ring_index(place - step if way == 0 else place + step, count)
        ref = stored.at[owner, :, pl.ds(half * rows, rows), :]
        return remote(
            ref, ref, send.at[way, half, step], recv.at[way, half, step], "seq", neighbours[way]
        )

    lanes = [(way, half) for half in range(2) for way in range(2)]
    ending = pl.ds(query_ref.shape[0] - 16, 16)
    edges = [
        remote(ref.at[ending, :], edge_out.at[c], edge_send.at[c], edge_recv.at[c], "seq", after)
        for c, ref in ((0, query_ref), (1, grad_ref))
    ]
    for step in range(count // 2):
        for way, half in lanes:
            if step < hops[way][half]:
                if step > 0:
                    copy(way, half, step - 1).wait_recv()
                copy(way, half, step).start()
        if step == 0:
            for edge in edges:
                edge.start()
    for way, half in lanes:
        copy(way, half, hops[way][half] - 1).wait_recv()
    for r in range(picked_ref.shape[0]):
        picked_ref[r] = stored[pick_ref[0, r], pick_ref[1, r]]
    for edge in edges:
        edge.wait()
    for way, half in lanes:
        for step in range(hops[way][half]):
            copy(way, half, step).wait_send()


def gather_tiles(pick, shard, queries, grad_out, count):
    tiles, rows, part = shard.shape
    vmem = pl.BlockSpec(memory_space=pltpu.VMEM)
    return pl.pallas_call(
        functools.partial(gather_body, count),
        in_specs=[pl.BlockSpec(memory_space=pltpu.SMEM), vmem]
        + [pl.BlockSpec(memory_space=pltpu.HBM)] * 2,
        out_specs=[vmem, vmem],
        out_shape=[
            jax.ShapeDtypeStruct((pick.shape[1], rows, part), shard.dtype),
            jax.ShapeDtypeStruct((2, 16, queries.shape[1]), queries.dtype),
        ],
        scratch_shapes=[
            pltpu.VMEM((count, tiles, rows, part), shard.dtype),
            pltpu.SemaphoreType.DMA((2, 2, count // 2)),
            pltpu.SemaphoreType.DMA((2, 2, count // 2)),
            pltpu.SemaphoreType.DMA((2,)),
            pltpu.SemaphoreType.DMA((2,)),
        ],
        compiler_params=pltpu.CompilerParams(
            collective_id=0, has_side_effects=True, vmem_limit_bytes=32 << 20
        ),
    )(pick, shard, queries, grad_out)


def scatter_body(
    count, share_ref, mine_ref, qout, out_ref, qgrad_ref, buf, qin, send, recv, q_send, q_recv
):
    head = lax.axis_index("head")
    groups, parts, _, width = qout.shape
    others = [(head + d) % parts for d in range(1, parts)]
    me = lax.axis_index("seq")
    place = ring_place(me, count)
    neighbours = (ring_index(place + 1, count), ring_index(place - 1, count))
    meet([("seq", other) for other in neighbours] + [("head", other) for other in others])
    tiles, length, _ = out_ref.shape
    requests = mine_ref.shape[0]
    rows = length // 2

    def own(way, target, k):
        total = None
        for r in range(requests):
            piece = share_ref[target * tiles + k, r] * mine_ref[r, way * rows : (way + 1) * rows, :]
            total = piece if total is None else total + piece
        return total

    def target_of(way, step):
        return ring_index(place - 1 - step if way == 0 else place + 1 + step, count)

    def copy(way, step, k):
        return remote(
            buf.at[way, step, k],
            buf.at[way, step + 1, k],
            send.at[way, step, k],
            recv.at[way, step, k],
            "seq",
            neighbours[way],
        )

    def to_head(i, d):
        return remote(
            qout.at[i, others[d - 1]],
            qin.at[head, i],
            q_send.at[i, d - 1],
            q_recv.at[i, d - 1],
            "head",
            others[d - 1],
        )

    for k in range(tiles):
        for way in range(2):
            buf[way, 0, k] = own(way, target_of(way, 0), k)
            copy(way, 0, k).start()

    for i in range(groups):
        for d in range(1, parts):
            to_head(i, d).start()
        qgrad_ref[i, :, pl.ds(pl.multiple_of(head * width, width), width)] = qout[i, head]

    def step_body(step, carry):
        for k in range(tiles):
            for way in range(2):
                piece = own(way, target_of(way, step), k)
                copy(way, step - 1, k).wait_recv()
                buf[way, step, k] = buf[way, step, k] + piece
                copy(way, step, k).start()
        return carry

    lax.fori_loop(1, count - 1, step_body, 0)
    for i in range(groups):
        for d in range(1, parts):
            source = (head + parts - d) % parts
            to_head(i, d).wait_recv()
            columns = pl.ds(pl.multiple_of(source * width, width), width)
            qgrad_ref[i, :, columns] = qin[source, i]
    for k in range(tiles):
        for way in range(2):
            piece = own(way, me, k)
            copy(way, count - 2, k).wait_recv()
            out_ref[k, way * rows : (way + 1) * rows, :] = (buf[way, count - 1, k] + piece).astype(
                out_ref.dtype
            )

    def drain(step, carry):
        for k in range(tiles):
            for way in range(2):
                copy(way, step, k).wait_send()
        return carry

    lax.fori_loop(0, count - 1, drain, 0)
    for i in range(groups):
        for d in range(1, parts):
            to_head(i, d).wait_send()


def scatter_tiles(share, mine, qout, count, tiles):
    _, length, part = mine.shape
    groups, parts, segment, width = qout.shape
    vmem = pl.BlockSpec(memory_space=pltpu.VMEM)
    return pl.pallas_call(
        functools.partial(scatter_body, count),
        in_specs=[
            pl.BlockSpec(memory_space=pltpu.SMEM),
            vmem,
            vmem,
        ],
        out_specs=[vmem, vmem],
        out_shape=[
            jax.ShapeDtypeStruct((tiles, length, part), BF16),
            jax.ShapeDtypeStruct((groups, segment, parts * width), BF16),
        ],
        scratch_shapes=[
            pltpu.VMEM((2, count, tiles, length // 2, part), F32),
            pltpu.VMEM((parts, groups, segment, width), BF16),
            pltpu.SemaphoreType.DMA((2, count - 1, tiles)),
            pltpu.SemaphoreType.DMA((2, count - 1, tiles)),
            pltpu.SemaphoreType.DMA((groups, parts - 1)),
            pltpu.SemaphoreType.DMA((groups, parts - 1)),
        ],
        compiler_params=pltpu.CompilerParams(
            collective_id=2, has_side_effects=True, vmem_limit_bytes=32 << 20
        ),
    )(share, mine, qout)


def group_body(
    parts, count, picked_ref, weight_ref, query_hbm, grad_hbm, edge_ref,
    att_ref, qout, out_ref,
    query_ref, grad_ref, load_sem, feat, kv, kv_grad, rows_in, tail, att_rows, qgrad_rows, edge_out, edge_in,
    term, from_core, across, from_chip,
    pick_send, pick_recv, far_send, far_recv, pass_send, pass_recv,
    edge_send, edge_recv, core_send, core_recv, chip_send, chip_recv,
):
    head = lax.axis_index("head")
    seq = lax.axis_index("seq")
    loads = [
        pltpu.make_async_copy(query_hbm, query_ref, load_sem.at[0]),
        pltpu.make_async_copy(grad_hbm, grad_ref, load_sem.at[1]),
    ]
    for load in loads:
        load.start()
    core, chip = head % 2, head // 2
    chips = parts // 2
    sibling = chip * 2 + 1 - core
    peers = [((chip + d) % chips) * 2 + core for d in range(1, chips)]
    before = (seq + count - 1) % count
    after = (seq + 1) % count
    meet([("head", other) for other in [sibling] + peers] + [("seq", before), ("seq", after)])
    part = picked_ref.shape[2]
    width = query_ref.shape[1]
    groups = query_ref.shape[0] // SPAN
    segment = SPAN // parts

    def to_sibling(i):
        return remote(
            picked_ref.at[i], feat.at[head, i], pick_send.at[i], pick_recv.at[i], "head", sibling
        )

    def to_far(i, d):
        return remote(
            picked_ref.at[i],
            feat.at[head, i],
            far_send.at[i, d - 1],
            far_recv.at[i, d - 1],
            "head",
            peers[d - 1],
        )

    def pass_far(i, d):
        ref = feat.at[((chip + chips - d) % chips) * 2 + core, i]
        return remote(
            ref, ref, pass_send.at[i, d - 1], pass_recv.at[i, d - 1], "head", sibling
        )

    def hand_over(i):
        for d in range(1, chips):
            to_far(i, d).wait_recv()
            pass_far(i, d).start()

    def to_core(i, d):
        target = (chip + d) % chips
        return remote(
            term.at[i, 1 - core, target],
            from_core.at[i, target],
            core_send.at[i, d],
            core_recv.at[i, d],
            "head",
            sibling,
        )

    def to_chip(i, d):
        return remote(
            across.at[i, d - 1],
            from_chip.at[i, d - 1],
            chip_send.at[i, d - 1],
            chip_recv.at[i, d - 1],
            "head",
            peers[d - 1],
        )

    edge = remote(edge_out, edge_in, edge_send.at[0], edge_recv.at[0], "seq", before)

    def pass_on(i):
        for d in range(1, chips):
            target = (chip + d) % chips
            to_core(i, d).wait_recv()
            across[i, d - 1] = term[i, core, target] + from_core[i, target]
            to_chip(i, d).start()

    last16 = lax.broadcasted_iota(jnp.int32, (16, width), 0) == 15
    last_segment = lax.broadcasted_iota(jnp.int32, (segment, width), 0) == segment - 1
    place = lax.broadcasted_iota(jnp.int32, (SPAN, width), 0)

    def finish_span(i, att16, qgrad16):
        rows = pl.ds(pl.multiple_of(i * SPAN + SPAN - 16, 16), 16)
        att_ref[rows, :] = jnp.where(last16, att16, att_ref[rows, :].astype(F32)).astype(BF16)
        qout[i, parts - 1] = jnp.where(
            last_segment, qgrad16[16 - segment :], qout[i, parts - 1].astype(F32)
        ).astype(BF16)

    for i in range(groups):
        for d in range(1, chips):
            to_far(i, d).start()
        to_sibling(i).start()
    for i in range(groups):
        feat[head, i] = picked_ref[i]
    tail[...] = edge_ref[...]
    for load in loads:
        load.wait()
    hand_over(0)

    def group(i, carry):
        tokens = pl.ds(pl.multiple_of(i * SPAN, SPAN), SPAN)
        limit = jnp.where(jnp.logical_and(seq == 0, i == 0), SPAN - 1, 0)
        for c, ref in ((0, query_ref), (1, grad_ref)):
            rows = ref[tokens, :].astype(F32)
            ending = jnp.where(last16, tail[c].astype(F32), rows[SPAN - 16 :])
            tail[c] = rows[SPAN - 16 :].astype(BF16)
            rows = jnp.concatenate([rows[: SPAN - 16], ending], 0)
            rows_in[c] = jnp.where(place >= limit, rows, 0.0).astype(BF16)
        to_sibling(i).wait_recv()
        for d in range(1, chips):
            pass_far(i, d).wait_recv()
        for c in range(2):
            total = None
            for j in range(parts):
                piece = dot(feat[j, i], weight_ref[c, j * part : (j + 1) * part, :], 1, 0)
                total = piece if total is None else total + piece
            kv[c] = total.astype(BF16)

        @pl.when(i + 1 < groups)
        def _():
            hand_over(i + 1)

        for h in range(width // HEAD_DIM):
            cols = slice(h * HEAD_DIM, (h + 1) * HEAD_DIM)
            q = rows_in[0, :, cols]
            g = rows_in[1, :, cols]
            k = kv[0, :, cols]
            v = kv[1, :, cols]
            scores = dot(q, k, 1, 1) * SCALE
            dprob = dot(g, v, 1, 1)
            expo = jnp.exp(scores - jnp.max(scores, axis=-1, keepdims=True))
            probs = expo / jnp.sum(expo, axis=-1, keepdims=True)
            half = probs.astype(BF16)
            delta = jnp.sum(probs * dprob, axis=-1, keepdims=True)
            dscore = (probs * (dprob - delta)).astype(BF16)
            att_rows[:, cols] = dot(half, v, 1, 0)
            qgrad_rows[:, cols] = dot(dscore, k, 1, 0) * SCALE
            kv_grad[0, :, cols] = (dot(dscore, q, 0, 0) * SCALE).astype(BF16)
            kv_grad[1, :, cols] = dot(half, g, 0, 0).astype(BF16)
        for d in [*range(1, chips), 0]:
            target = (chip + d) % chips
            for c in (1 - core, core):
                first = (target * 2 + c) * part
                rows = pl.ds(pl.multiple_of(first, part), part)
                term[i, c, target] = dot(kv_grad[0], weight_ref[0, rows, :], 1, 1) + dot(
                    kv_grad[1], weight_ref[1, rows, :], 1, 1
                )
                if c is not core:
                    to_core(i, d).start()
        att = jnp.where(place >= limit, att_rows[...], 0.0)
        att_ref[tokens, :] = att.astype(BF16)
        for j in range(parts):
            qout[i, j] = qgrad_rows[j * segment : (j + 1) * segment, :].astype(BF16)

        @pl.when(i == 0)
        def _():
            edge_out[0] = att_rows[SPAN - 16 :, :].astype(BF16)
            edge_out[1] = qgrad_rows[SPAN - 16 :, :].astype(BF16)
            edge.start()

        @pl.when(i > 0)
        def _():
            finish_span(i - 1, att_rows[SPAN - 16 :, :], qgrad_rows[SPAN - 16 :, :])

        pass_on(i)
        return carry

    lax.fori_loop(0, groups, group, 0)
    edge.wait_recv()
    finish_span(groups - 1, edge_in[0].astype(F32), edge_in[1].astype(F32))
    for i in range(groups):
        to_core(i, 0).wait_recv()
        total = term[i, core, chip] + from_core[i, chip]
        for d in range(1, chips):
            to_chip(i, d).wait_recv()
            total = total + from_chip[i, d - 1]
        out_ref[i * WINDOW : (i + 1) * WINDOW, :] = total
    edge.wait_send()
    for i in range(groups):
        for d in range(chips):
            to_core(i, d).wait_send()
        to_sibling(i).wait_send()
        for d in range(1, chips):
            to_chip(i, d).wait_send()
            to_far(i, d).wait_send()
            pass_far(i, d).wait_send()


def run_groups(picked, kv_weight, queries, grad_out, edge, parts, count):
    groups, rows, part = picked.shape
    token_rows, width = queries.shape
    chips = parts // 2
    segment = SPAN // parts
    vmem = pl.BlockSpec(memory_space=pltpu.VMEM)
    hbm = pl.BlockSpec(memory_space=pltpu.HBM)
    dma = pltpu.SemaphoreType.DMA
    return pl.pallas_call(
        functools.partial(group_body, parts, count),
        in_specs=[vmem, vmem, hbm, hbm, vmem],
        out_specs=[vmem] * 3,
        out_shape=[
            jax.ShapeDtypeStruct((token_rows, width), BF16),
            jax.ShapeDtypeStruct((groups, parts, segment, width), BF16),
            jax.ShapeDtypeStruct((groups * WINDOW, part), F32),
        ],
        scratch_shapes=[
            pltpu.VMEM((token_rows, width), BF16),
            pltpu.VMEM((token_rows, width), BF16),
            dma((2,)),
            pltpu.VMEM((parts, groups, WINDOW, part), BF16),
            pltpu.VMEM((2, WINDOW, width), BF16),
            pltpu.VMEM((2, WINDOW, width), BF16),
            pltpu.VMEM((2, SPAN, width), BF16),
            pltpu.VMEM((2, 16, width), BF16),
            pltpu.VMEM((SPAN, width), F32),
            pltpu.VMEM((SPAN, width), F32),
            pltpu.VMEM((2, 16, width), BF16),
            pltpu.VMEM((2, 16, width), BF16),
            pltpu.VMEM((groups, 2, chips, WINDOW, part), F32),
            pltpu.VMEM((groups, chips, WINDOW, part), F32),
            pltpu.VMEM((groups, chips - 1, WINDOW, part), F32),
            pltpu.VMEM((groups, chips - 1, WINDOW, part), F32),
            dma((groups,)),
            dma((groups,)),
            dma((groups, chips - 1)),
            dma((groups, chips - 1)),
            dma((groups, chips - 1)),
            dma((groups, chips - 1)),
            dma((1,)),
            dma((1,)),
            dma((groups, chips)),
            dma((groups, chips)),
            dma((groups, chips - 1)),
            dma((groups, chips - 1)),
        ],
        compiler_params=pltpu.CompilerParams(
            collective_id=1, has_side_effects=True, vmem_limit_bytes=48 << 20
        ),
    )(picked, kv_weight, queries, grad_out, edge)


def per_device(queries, encodings, kv_weight, grad_out, neighbour_owner, neighbour_slot):
    seq_count = lax.axis_size("seq")
    seq_index = lax.axis_index("seq")
    parts = lax.axis_size("head")
    token_rows, width = queries.shape
    requests = token_rows // SPAN * NEIGHBOURS
    tile_rows, _, part = encodings.shape

    pick = jnp.stack([neighbour_owner, neighbour_slot], 0)
    pick = jnp.roll(pick, 1, axis=1).reshape(2, seq_count, requests)
    pick = lax.dynamic_index_in_dim(pick, seq_index, 1, keepdims=False)
    queries = pltpu.with_memory_space_constraint(queries, pltpu.HBM)
    grad_out = pltpu.with_memory_space_constraint(grad_out, pltpu.HBM)
    picked, edge = gather_tiles(pick, encodings, queries, grad_out, seq_count)
    picked = picked.reshape(requests // NEIGHBOURS, WINDOW, part)
    attended, qout, mine = run_groups(
        picked, kv_weight, queries, grad_out, edge, parts, seq_count
    )
    mine = mine.reshape(requests, NEIGHBOUR_LEN, part)
    tile = pick[0] * tile_rows + pick[1]
    share = (jnp.arange(seq_count * tile_rows)[:, None] == tile[None, :]).astype(F32)
    total, query_grad = scatter_tiles(share, mine, qout, seq_count, tile_rows)
    return attended, query_grad, total


def solution(mesh):
    in_specs = (
        P("seq", "head"),
        P("seq", None, "head"),
        P(None, None, "head"),
        P("seq", "head"),
        P(),
        P(),
    )
    out_specs = (P("seq", "head"), P("seq", "head", None), P("seq", None, "head"))
    return jax.shard_map(
        per_device, mesh=mesh, in_specs=in_specs, out_specs=out_specs, check_vma=False
    )
```
